32 devices in a mesh: gx: 8 (over z, core), gy: 4 (over y, x).
Axes of the slice: x: 2, y: 2, z: 4, core: 2. Of those that a mesh axis runs over, the one named last changes fastest.
Arguments:
- density: float32 [128, 192, 128], P('gx', 'gy'), may hold values from -6 to 6
- momenta: float32 [3, 128, 192, 128], P(None, 'gx', 'gy'), may hold values from -6 to 6
- smooth_taps: float32 [33], replicated, may hold values from -1 to 1
- deriv_taps: float32 [33], replicated, may hold values from -1 to 1
- kick_step: float32 [], replicated, may hold values from 0.5 to 1.5
Outputs:
- kicked: float32 [3, 128, 192, 128], P(None, 'gx', 'gy')
The draws below stay inside these ranges and needn't reach their ends.
All inputs are finite; a program needn't handle non-finite values.
Results may differ from the reference program's by a relative error of at most 0.00007.
Values sent between devices are 32-bit elements; how exact they have to be, the bound alone decides.
No kernel may reach another device: no remote copies, remote signals or barrier semaphores. Data moves between devices by JAX's collectives and lax.ppermute only.
A program may use at most 64 MiB of HBM per device.

```python
import jax
import jax.numpy as jnp
from jax import lax

NZ = 128
RADIUS = 16
FACTOR = 4
NX = 128
NY = 192
CNX = 32
CNY = 48
CNZ = 32


def level_of(key, extent, split, smallest, high):
    gain, own = 1.0, jax.random.fold_in(key, 6)
    for dim, blocks in split:
        steps = jnp.exp(jax.random.uniform(jax.random.fold_in(own, dim), (blocks,), jnp.float32, smallest / len(split), high / len(split)))
        gain = gain * jnp.repeat(steps, extent[dim] // blocks).reshape([-1 if axis == dim else 1 for axis in range(len(extent))])
    return gain


def noise(stream_key, extent, scale, most, shards=(), held_as=jnp.bfloat16):
    drawn = jax.random.normal(stream_key, extent, jnp.float32) * scale
    if len(shards) > 0:
        drawn = level_of(stream_key, extent, shards, -0.22, 0.18) * drawn
    return jnp.clip(drawn, min=-most, max=most).astype(held_as)


def setup_inputs(seed: int = 0) -> dict:
    seeds = jax.random.split(jax.random.key(seed), 6)
    density = noise(seeds[0], (NX, NY, NZ), 1.0, 6.0, ((0, 8), (1, 4)), jnp.float32)
    momenta = noise(seeds[1], (3, NX, NY, NZ), 1.0, 6.0, ((1, 8), (2, 4)), jnp.float32)
    smooth_taps = noise(seeds[2], (2 * RADIUS + 1,), (2 * RADIUS + 1) ** -0.5, 1.0, (), jnp.float32)
    deriv_taps = noise(seeds[3], (2 * RADIUS + 1,), (2 * RADIUS + 1) ** -0.5, 1.0, (), jnp.float32)
    kick_step = jnp.clip(jax.random.uniform(seeds[4], (), jnp.float32, 0.5, 1.5), 0.5, 1.5)
    return {"density": density, "momenta": momenta, "smooth_taps": smooth_taps, "deriv_taps": deriv_taps, "kick_step": kick_step}


LONG_COUPLING = 16.0


def convolve(field, weights, along):
    def add_tap(tap_step, total):
        return total + weights[tap_step] * jnp.roll(field, RADIUS - tap_step, along)
    return lax.fori_loop(0, 2 * RADIUS + 1, add_tap, jnp.zeros_like(field))


def long_forces(density):
    coarse = density.reshape(CNX, FACTOR, CNY, FACTOR, CNZ, FACTOR).mean(axis=(1, 3, 5))
    spectrum = jnp.fft.fftn(coarse)
    phase_x = 2.0 * jnp.pi * jnp.arange(CNX) / CNX
    phase_y = 2.0 * jnp.pi * jnp.arange(CNY) / CNY
    phase_z = 2.0 * jnp.pi * jnp.arange(CNZ) / CNZ
    laplace = (2.0 - 2.0 * jnp.cos(phase_x))[:, None, None] + (2.0 - 2.0 * jnp.cos(phase_y))[None, :, None] + (2.0 - 2.0 * jnp.cos(phase_z))[None, None, :]
    anchor = laplace.shape[0] * 0
    safe = laplace.at[anchor, anchor, anchor].set(1.0)
    inverse = (1.0 / safe).at[anchor, anchor, anchor].set(0.0)
    sine_list = [jnp.sin(phase_x)[:, None, None], jnp.sin(phase_y)[None, :, None], jnp.sin(phase_z)[None, None, :]]
    return [jnp.real(jnp.fft.ifftn(1j * sine_part * spectrum * inverse)) for sine_part in sine_list]


def reference(density, momenta, smooth_taps, deriv_taps, kick_step):
    smooth_x = convolve(density, smooth_taps, 0)
    deriv_x = convolve(density, deriv_taps, 0)
    smooth_xy = convolve(smooth_x, smooth_taps, 1)
    short_range = [convolve(convolve(deriv_x, smooth_taps, 1), smooth_taps, 2),
                   convolve(convolve(smooth_x, deriv_taps, 1), smooth_taps, 2),
                   convolve(smooth_xy, deriv_taps, 2)]
    long_range = long_forces(density)
    kicked = []
    for component in range(3):
        fine_long = jnp.repeat(jnp.repeat(jnp.repeat(long_range[component], FACTOR, 0), FACTOR, 1), FACTOR, 2)
        kicked.append(momenta[component] + kick_step * (short_range[component] + LONG_COUPLING * fine_long))
    return jnp.stack(kicked)
```

```python
import functools
import math

import jax
import jax.numpy as jnp
import numpy as np
from jax import lax
from jax.experimental import pallas as pl
from jax.experimental.pallas import tpu as pltpu
from jax.sharding import PartitionSpec as P

FACTOR = 4
LANES = 128
LONG_COUPLING = 16.0
HIGHEST = lax.Precision.HIGHEST
VMEM = pl.BlockSpec(memory_space=pltpu.VMEM)
SMEM = pl.BlockSpec(memory_space=pltpu.SMEM)


def real_basis(count):
    places = np.arange(count, dtype=np.float64)
    rows, waves = [np.full(count, 1.0 / math.sqrt(count))], [0]
    for wave in range(1, (count + 1) // 2):
        phase = 2.0 * math.pi * wave * places / count
        rows += [math.sqrt(2.0 / count) * np.cos(phase), math.sqrt(2.0 / count) * np.sin(phase)]
        waves += [wave, wave]
    if count % 2 == 0:
        rows.append(np.cos(math.pi * places) / math.sqrt(count))
        waves.append(count // 2)
    return np.stack(rows), np.array(waves)


def centred(basis):
    return 0.5 * (np.roll(basis, -1, 1) - np.roll(basis, 1, 1))


def eigenvalues(waves, count):
    return 2.0 - 2.0 * np.cos(2.0 * math.pi * waves / count)


def f32(table):
    return jnp.asarray(np.asarray(table, dtype=np.float32))


def split(values):
    high = values.astype(jnp.bfloat16)
    low = (values - high.astype(jnp.float32)).astype(jnp.bfloat16)
    return high, low


def dot3(left, right):
    left_high, left_low = split(left)
    right_high, right_low = split(right)
    return jnp.dot(
        jnp.concatenate([left_high, left_high, left_low], axis=1),
        jnp.concatenate([right_high, right_low, right_high], axis=0),
        preferred_element_type=jnp.float32,
    )


def prepare_kernel(density, pool_table, turned, head, tail, coarse, pooled):
    rows, cols, depth = density.shape
    radius = head.shape[0]
    groups, lines = rows // FACTOR, cols // FACTOR
    for col in range(cols):
        strip = density[:, col, :]
        turned[col] = strip
        if col < radius:
            head[col] = strip
        if col >= cols - radius:
            tail[col - (cols - radius)] = strip
    for group in range(groups):
        total = density[FACTOR * group]
        for step in range(1, FACTOR):
            total = total + density[FACTOR * group + step]
        pooled[group * cols : (group + 1) * cols, :] = total
    parts = []
    for group in range(groups):
        total = pooled[pl.ds(group * cols, lines, stride=FACTOR), :]
        for step in range(1, FACTOR):
            total = total + pooled[pl.ds(group * cols + step, lines, stride=FACTOR), :]
        parts.append(total)
    result = jnp.dot(
        jnp.concatenate(parts, axis=1), pool_table[...],
        preferred_element_type=jnp.float32, precision=HIGHEST,
    )
    for copy in range(coarse.shape[0]):
        coarse[copy, 0:lines, :] = result
        coarse[copy, lines:, :] = jnp.zeros((coarse.shape[1] - lines, LANES), jnp.float32)


def bands_kernel(smooth, deriv, parity, along_x, along_y, smooth_z, deriv_z, *, radius):
    taps = 2 * radius + 1
    odd = parity[0]

    def banded(offset):
        pair = [jnp.zeros(offset.shape, jnp.float32)] * 2
        for tap in range(taps):
            here = offset == tap
            pair = [jnp.where(here, w[tap], m) for w, m in zip((smooth, deriv), pair)]
        return pair

    rows = along_x.shape[0] // 2
    shape = (rows, 3 * rows)
    target = lax.broadcasted_iota(jnp.int32, shape, 0)
    source = lax.broadcasted_iota(jnp.int32, shape, 1)
    side = jnp.where(odd == 1, -1, 1)
    place = jnp.where(
        source < rows, source,
        jnp.where(source < 2 * rows, source - rows + side * rows, source - 2 * rows - side * rows),
    )
    matrix = jnp.concatenate(banded(place - target + radius), axis=0)
    high, low = split(matrix)
    along_x[...] = jnp.concatenate([high, low, high], axis=1)

    cols = along_y.shape[0] // 2
    shape = (cols, cols + 2 * radius)
    target = lax.broadcasted_iota(jnp.int32, shape, 0)
    source = lax.broadcasted_iota(jnp.int32, shape, 1)
    place = jnp.where(
        source < cols, source,
        jnp.where(source < cols + radius, source - cols - radius, source - radius),
    )
    matrix = jnp.concatenate(banded(place - target + radius), axis=0)
    high, low = split(matrix)
    along_y[...] = jnp.concatenate([high, low, high], axis=1)

    depth = smooth_z.shape[1]
    source = lax.broadcasted_iota(jnp.int32, (depth, depth), 0)
    target = lax.broadcasted_iota(jnp.int32, (depth, depth), 1)
    offset = source - target + radius
    offset = jnp.where(offset < 0, offset + depth, offset)
    offset = jnp.where(offset >= depth, offset - depth, offset)
    for ref, matrix in zip((smooth_z, deriv_z), banded(offset)):
        high, low = split(matrix)
        ref[...] = jnp.concatenate([high, low, high], axis=0)


def first_kernel(blocks, table, spectrum, *, lines):
    count, padded, _ = blocks.shape
    spins = LANES // (LANES // FACTOR)
    quads = spectrum.shape[1] // lines

    def quad(index, carry):
        def block(other, total):
            values = blocks[other]
            for spin in range(spins):
                weights = table[(index * count + other) * spins + spin]
                turned = values if spin == 0 else pltpu.roll(values, LANES - spin * (LANES // spins), 1)
                total = total + turned * weights
            return total
        total = lax.fori_loop(0, count, block, jnp.zeros((padded, LANES), jnp.float32), unroll=count <= 8)
        for copy in range(spectrum.shape[0]):
            spectrum[copy, pl.ds(index * lines, lines), :] = total[:lines]
        return carry

    lax.fori_loop(0, quads, quad, 0, unroll=quads <= 8)


def solve_kernel(
    spectra, forward, inverse, inverse_x, second_values, other_values, inverse_z, force,
    gathered, back, columns, *, lines,
):
    count, rows, _ = spectra.shape
    quads = rows // lines
    fine = inverse.shape[0] // 2
    groups = force.shape[1]

    def gather(index, carry):
        for block in range(count):
            gathered[pl.ds(block * lines, lines), :] = spectra[block, pl.ds(index * lines, lines), :]
        values = dot3(forward[...], gathered[...])
        total = second_values[...] + other_values[index]
        scale = jnp.where(total > 0.0, 1.0 / jnp.where(total > 0.0, total, 1.0), 0.0)
        back[index] = dot3(inverse[...], values * scale)
        return carry

    lax.fori_loop(0, quads, gather, 0, unroll=quads <= 8)

    for group in range(groups):
        def collect(index, totals):
            whole = back[index]
            value, slope = whole[:fine], whole[fine:]
            along = inverse_x[(index * 2) * groups + group]
            along_slope = inverse_x[(index * 2 + 1) * groups + group]
            return (
                totals[0] + value * along_slope, totals[1] + slope * along, totals[2] + value * along,
            )
        zero = jnp.zeros((fine, LANES), jnp.float32)
        totals = lax.fori_loop(0, quads, collect, (zero, zero, zero), unroll=quads <= 8)
        for component in range(3):
            columns[component, group * fine : (group + 1) * fine, :] = totals[component]
    for component in range(3):
        table = inverse_z[1] if component == 2 else inverse_z[0]
        result = dot3(columns[component], table)
        for group in range(groups):
            force[component, group] = result[group * fine : (group + 1) * fine]


def kick_kernel(
    own, swapped, crossed, left, right, swapped_sides, cross_left, cross_right,
    along_x, along_y, smooth_z, deriv_z, force, momenta, step, kicked, smooth_x, deriv_x, *, group,
):
    cols, rows, depth = own.shape
    radius = left.shape[0]
    wide = cols + 2 * radius

    def first(col, parts):
        high, low = split(jnp.concatenate(parts, axis=0))
        return jnp.concatenate([high, high, low], axis=0)

    def store(col, result):
        smooth_x[pl.ds(col, rows, stride=wide), :] = result[:rows]
        deriv_x[pl.ds(col, rows, stride=wide), :] = result[rows:]

    def pair(cols_of, parts_of):
        stacked = jnp.concatenate([first(c, p) for c, p in zip(cols_of, parts_of)], axis=1)
        result = jnp.dot(along_x[...], stacked, preferred_element_type=jnp.float32)
        for at, col in enumerate(cols_of):
            store(col, result[:, at * depth : (at + 1) * depth])

    for col in range(0, cols, 2):
        pair((col, col + 1), [[own[c], swapped[c], crossed[c]] for c in (col, col + 1)])
    for col in range(radius):
        pair(
            (cols + col, cols + radius + col),
            [
                [left[col], swapped_sides[col], cross_left[col]],
                [right[col], swapped_sides[radius + col], cross_right[col]],
            ],
        )

    scale = step[0]
    for start in range(0, rows, group):
        pieces = [[], [], []]
        for row in range(start, start + group):
            values = jnp.concatenate(
                [smooth_x[row * wide : (row + 1) * wide, :], deriv_x[row * wide : (row + 1) * wide, :]], axis=1
            )
            high, low = split(values)
            result = jnp.dot(
                along_y[...], jnp.concatenate([high, high, low], axis=0), preferred_element_type=jnp.float32
            )
            for at, piece in enumerate(
                (result[:cols, depth:], result[cols:, :depth], result[:cols, :depth])
            ):
                high, low = split(piece)
                pieces[at].append(jnp.concatenate([high, high, low], axis=1))
        smooth = jnp.dot(
            jnp.concatenate(pieces[0] + pieces[1], axis=0), smooth_z[...], preferred_element_type=jnp.float32
        )
        deriv = jnp.dot(jnp.concatenate(pieces[2], axis=0), deriv_z[...], preferred_element_type=jnp.float32)
        for at in range(group):
            row = start + at
            for component in range(3):
                if component < 2:
                    base = (component * group + at) * cols
                    short = smooth[base : base + cols]
                else:
                    short = deriv[at * cols : (at + 1) * cols]
                kicked[component, row] = momenta[component, row] + scale * (
                    short + force[component, row // FACTOR]
                )


def call(body, outs, name, scratch=(), cost=None, smem=(), n_in=0):
    return pl.pallas_call(
        body,
        out_shape=[jax.ShapeDtypeStruct(s, d) for s, d in outs],
        in_specs=[SMEM if at in smem else VMEM for at in range(n_in)],
        out_specs=[VMEM for _ in outs],
        scratch_shapes=list(scratch),
        name=name,
        cost_estimate=cost,
        compiler_params=pltpu.CompilerParams(vmem_limit_bytes=56 * 1024 * 1024),
    )


def per_device(density, momenta, smooth_taps, deriv_taps, kick_step):
    rows, cols, depth = density.shape
    radius = (smooth_taps.shape[0] - 1) // 2
    count_gx, count_gy = lax.axis_size("gx"), lax.axis_size("gy")
    assert rows == radius and count_gx % 2 == 0 and cols >= radius and depth == LANES
    groups, lines, deep = rows // FACTOR, cols // FACTOR, depth // FACTOR
    assert groups == FACTOR and groups * deep == LANES
    coarse_x, coarse_y = groups * count_gx, lines * count_gy
    padded = -(-lines // 8) * 8
    f, b = jnp.float32, jnp.bfloat16
    gx, gy = lax.axis_index("gx"), lax.axis_index("gy")

    basis_x, waves_x = real_basis(coarse_x)
    basis_y, waves_y = real_basis(coarse_y)
    basis_z, waves_z = real_basis(deep)

    pool = np.zeros((groups * depth, LANES))
    for group in range(groups):
        for cell in range(depth):
            pool[group * depth + cell, group * deep : (group + 1) * deep] = (
                basis_z[:, cell // FACTOR] / FACTOR**3
            )
    turned, head, tail, coarse = call(
        prepare_kernel,
        [((cols, rows, depth), f), ((radius, rows, depth), f), ((radius, rows, depth), f),
         ((count_gx, padded, LANES), f)],
        "prepare", [pltpu.VMEM((groups * cols, depth), f)], n_in=2,
        cost=pl.CostEstimate(flops=10**6, bytes_accessed=10**6, transcendentals=0),
    )(density, f32(pool))

    def shift(values, pairs):
        return lax.ppermute(values, ("gx", "gy"), [
            (a * count_gy + c, d * count_gy + e) for (a, c), (d, e) in pairs
        ])

    every = [(i, j) for i in range(count_gx) for j in range(count_gy)]
    beside = lambda i: i + 1 if i % 2 == 0 else i - 1
    across = lambda i: (i - 1) % count_gx if i % 2 == 0 else (i + 1) % count_gx
    crossed = shift(turned, [((i, j), (across(i), j)) for i, j in every])
    swapped = shift(turned, [((i, j), (beside(i), j)) for i, j in every])
    left = shift(tail, [((i, j), (i, (j + 1) % count_gy)) for i, j in every])
    right = shift(head, [((i, j), (i, (j - 1) % count_gy)) for i, j in every])
    cross_left = shift(tail, [((i, j), (across(i), (j + 1) % count_gy)) for i, j in every])
    cross_right = shift(head, [((i, j), (across(i), (j - 1) % count_gy)) for i, j in every])

    blocks = lax.all_to_all(coarse, "gx", split_axis=0, concat_axis=0, tiled=True)

    along_x, along_y, smooth_z, deriv_z = call(
        functools.partial(bands_kernel, radius=radius),
        [((2 * rows, 9 * rows), b), ((2 * cols, 3 * (cols + 2 * radius)), b),
         ((3 * depth, depth), b), ((3 * depth, depth), b)],
        "bands", smem=(0, 1, 2), n_in=3,
        cost=pl.CostEstimate(flops=10**6, bytes_accessed=10**6, transcendentals=0),
    )(smooth_taps, deriv_taps, (gx % 2).astype(jnp.int32).reshape(1))

    quads = coarse_x // groups
    spread = np.zeros((quads, count_gx, groups, groups, deep))
    for turn in range(groups):
        for j in range(groups):
            for quad in range(quads):
                spread[quad, :, turn, j, :] = basis_x[quad * groups + j].reshape(count_gx, groups)[
                    :, (j + turn) % groups
                ][:, None]
    (spectrum,) = call(
        functools.partial(first_kernel, lines=lines),
        [((count_gy, quads * lines, LANES), f)], "first", n_in=2,
        cost=pl.CostEstimate(flops=10**6, bytes_accessed=10**6, transcendentals=0),
    )(blocks, f32(spread.reshape(-1, 1, LANES)))
    spectra = lax.all_to_all(spectrum, "gy", split_axis=0, concat_axis=0, tiled=True)

    back_y = np.concatenate([
        np.repeat(t.T.reshape(count_gy, lines, coarse_y), FACTOR, 1) for t in (basis_y, centred(basis_y))
    ], 1)
    back_x = np.stack([basis_x, centred(basis_x)])
    back_x = back_x.reshape(2, quads, groups, count_gx, groups).transpose(3, 1, 0, 4, 2)
    back_x = np.repeat(back_x[..., None], deep, -1).reshape(count_gx, quads * 2 * groups, 1, LANES)
    back_z = np.stack([
        np.tile(np.repeat(t, FACTOR, 1), (groups, 1)) * LONG_COUPLING for t in (basis_z, centred(basis_z))
    ])
    other = (
        eigenvalues(waves_x, coarse_x).reshape(quads, 1, groups, 1) + eigenvalues(waves_z, deep)
    ).reshape(quads, 1, LANES)
    second = np.repeat(eigenvalues(waves_y, coarse_y)[:, None], LANES, 1)
    (force,) = call(
        functools.partial(solve_kernel, lines=lines),
        [((3, groups, cols, depth), f)], "solve",
        [pltpu.VMEM((coarse_y, LANES), f), pltpu.VMEM((quads, 2 * cols, LANES), f),
         pltpu.VMEM((3, groups * cols, LANES), f)], n_in=7,
        cost=pl.CostEstimate(flops=10**6, bytes_accessed=10**6, transcendentals=0),
    )(
        spectra, f32(basis_y), f32(back_y)[gy], f32(back_x)[gx], f32(second), f32(other), f32(back_z),
    )

    swapped_sides = shift(
        jnp.concatenate([left, right], 0), [((i, j), (beside(i), j)) for i, j in every]
    )
    wide = cols + 2 * radius
    (kicked,) = call(
        functools.partial(kick_kernel, group=4),
        [((3, rows, cols, depth), f)], "kick",
        [pltpu.VMEM((rows * wide, depth), f), pltpu.VMEM((rows * wide, depth), f)], n_in=15, smem=(14,),
        cost=pl.CostEstimate(flops=10**9, bytes_accessed=5 * 10**6, transcendentals=0),
    )(
        turned, swapped, crossed, left, right, swapped_sides, cross_left, cross_right,
        along_x, along_y, smooth_z, deriv_z, force, momenta, kick_step.reshape(1),
    )
    return kicked


def solution(mesh):
    in_specs = (P("gx", "gy", None), P(None, "gx", "gy", None), P(), P(), P())
    out_specs = P(None, "gx", "gy", None)
    return jax.shard_map(
        per_device, mesh=mesh, in_specs=in_specs, out_specs=out_specs, check_vma=False
    )
```

```python
import functools
import math

import jax
import jax.numpy as jnp
import ml_dtypes
import numpy as np
from jax import lax
from jax.experimental import pallas as pl
from jax.experimental.pallas import tpu as pltpu
from jax.sharding import PartitionSpec as P


FACTOR = 4
LANES = 128
CHUNK = 8
GROUP = 8
LONG_COUPLING = 16.0
VMEM = pl.BlockSpec(memory_space=pltpu.VMEM)
SMEM = pl.BlockSpec(memory_space=pltpu.SMEM)
HBM = pl.BlockSpec(memory_space=pltpu.HBM)
DMA = pltpu.SemaphoreType.DMA


def real_basis(count):
    places = np.arange(count, dtype=np.float64)
    rows, waves = [np.full(count, 1.0 / math.sqrt(count))], [0]
    for wave in range(1, (count + 1) // 2):
        phase = 2.0 * math.pi * wave * places / count
        rows += [math.sqrt(2.0 / count) * np.cos(phase), math.sqrt(2.0 / count) * np.sin(phase)]
        waves += [wave, wave]
    if count % 2 == 0:
        rows.append(np.cos(math.pi * places) / math.sqrt(count))
        waves.append(count // 2)
    return np.stack(rows), np.array(waves)


def centred(basis):
    return 0.5 * (np.roll(basis, -1, 1) - np.roll(basis, 1, 1))


def eigenvalues(waves, count):
    return 2.0 - 2.0 * np.cos(2.0 * math.pi * waves / count)


def split_table(table, axis):
    table = np.asarray(table, dtype=np.float32)
    high = table.astype(ml_dtypes.bfloat16)
    low = (table - high.astype(np.float32)).astype(ml_dtypes.bfloat16)
    return np.concatenate([high, low, high], axis)


def split(values):
    high = values.astype(jnp.bfloat16)
    low = (values - high.astype(jnp.float32)).astype(jnp.bfloat16)
    return high, low


def tripled(values, axis):
    high, low = split(values)
    return jnp.concatenate([high, high, low], axis=axis)


def dot(left, right):
    return jnp.dot(left, right, preferred_element_type=jnp.float32)


def prepare_kernel(density_far, pool_far, density, head, tail, coarse, pool_table, pooled, sems):
    rows, cols, _ = density.shape
    radius = head.shape[0]
    groups, lines = rows // FACTOR, cols // FACTOR
    copies = [
        pltpu.make_async_copy(
            density_far.at[pl.ds(FACTOR * group, FACTOR)], density.at[pl.ds(FACTOR * group, FACTOR)], sems.at[group]
        )
        for group in range(groups)
    ]
    copies.append(pltpu.make_async_copy(pool_far, pool_table, sems.at[groups]))
    for copy in copies:
        copy.start()
    for group in range(groups):
        copies[group].wait()
        total = density[FACTOR * group]
        for step in range(1, FACTOR):
            total = total + density[FACTOR * group + step]
        pooled[group * cols : (group + 1) * cols, :] = total
    parts = []
    for group in range(groups):
        total = pooled[pl.ds(group * cols, lines, stride=FACTOR), :]
        for step in range(1, FACTOR):
            total = total + pooled[pl.ds(group * cols + step, lines, stride=FACTOR), :]
        parts.append(total)
    copies[groups].wait()
    waves = dot(tripled(jnp.concatenate(parts, axis=0), 1), pool_table[...])
    lane_group = lax.broadcasted_iota(jnp.int32, (lines, LANES), 1) // (LANES // groups)
    result = waves[:lines]
    for group in range(1, groups):
        result = jnp.where(lane_group == group, waves[group * lines : (group + 1) * lines], result)
    result = jnp.concatenate([result, jnp.zeros((coarse.shape[1] - lines, LANES), jnp.float32)], axis=0)

    def spread_out(copy, carry):
        coarse[copy] = result
        return carry

    lax.fori_loop(0, coarse.shape[0], spread_out, 0, unroll=coarse.shape[0] <= 64)
    for col in range(radius):
        head[col] = density[:, col, :]
        tail[col] = density[:, cols - radius + col, :]


def band_rows(rows, cols, depth, radius):
    sizes = {
        "x": (2 * rows, 9 * rows), "own": (2 * cols, 3 * cols), "sides": (4 * radius, 6 * radius),
        "smooth": (3 * depth, depth), "deriv": (3 * depth, depth),
    }
    places, start = {}, 0
    for name, (height, width) in sizes.items():
        places[name] = (start, start + height, width)
        start += height
    return places


def band(bands, places, name):
    start, stop, width = places[name]
    return bands[start:stop, :width]


def bands_kernel(smooth_far, deriv_far, step, bands, scale, smooth, deriv, sems, *, rows, cols, depth, radius):
    copies = [
        pltpu.make_async_copy(smooth_far, smooth, sems.at[0]), pltpu.make_async_copy(deriv_far, deriv, sems.at[1]),
    ]
    for copy in copies:
        copy.start()
    scale[...] = jnp.full(scale.shape, step[...], jnp.float32)
    for copy in copies:
        copy.wait()
    taps = 2 * radius + 1
    odd = lax.axis_index("core")
    at = band_rows(rows, cols, depth, radius)

    def banded(offset):
        pair = [jnp.zeros(offset.shape, jnp.float32)] * 2
        for tap in range(taps):
            here = offset == tap
            pair = [jnp.where(here, w[tap], m) for w, m in zip((smooth, deriv), pair)]
        return pair

    def iotas(shape):
        return lax.broadcasted_iota(jnp.int32, shape, 0), lax.broadcasted_iota(jnp.int32, shape, 1)

    def left_factor(name, offset):
        high, low = split(jnp.concatenate(banded(offset), axis=0))
        start, stop, width = at[name]
        bands[start:stop, :width] = jnp.concatenate([high, low, high], axis=1)

    target, source = iotas((rows, 3 * rows))
    side = jnp.where(odd == 1, -1, 1)
    place = jnp.where(
        source < rows, source,
        jnp.where(source < 2 * rows, source - rows + side * rows, source - 2 * rows - side * rows),
    )
    left_factor("x", place - target + radius)

    target, source = iotas((cols, cols))
    left_factor("own", source - target + radius)
    target, source = iotas((2 * radius, 2 * radius))
    place = jnp.where(source < radius, source - radius, source - radius + cols)
    row = jnp.where(target < radius, target, target - 2 * radius + cols)
    left_factor("sides", place - row + radius)

    source, target = iotas((depth, depth))
    offset = source - target + radius
    offset = jnp.where(offset < 0, offset + depth, offset)
    offset = jnp.where(offset >= depth, offset - depth, offset)
    for name, matrix in zip(("smooth", "deriv"), banded(offset)):
        high, low = split(matrix)
        start, stop, width = at[name]
        bands[start:stop, :width] = jnp.concatenate([high, low, high], axis=0)


def solve_kernel(
    blocks, beside_blocks, spread, tables, own_tables, back_z, forward, inverse, force,
    gathered, turned, back, columns, *, lines,
):
    core = lax.axis_index("core")
    fine = force.shape[2]
    groups = force.shape[1]
    quads = back.shape[0]
    whole_y = gathered.shape[0]
    parts = whole_y // lines
    count = 2 * blocks.shape[0] // parts
    width = LANES // FACTOR
    few = count <= CHUNK

    def spin_block(pair, carry):
        for side, source in enumerate((blocks, beside_blocks)):
            for part in range(parts):
                gathered[part * lines : (part + 1) * lines, :LANES] = source[pair * parts + part, :lines, :]
            values = gathered[:, :LANES]
            place = (2 * pair + (core if side == 0 else 1 - core)) * FACTOR
            for spin in range(FACTOR):
                turned[place + spin] = values if spin == 0 else pltpu.roll(values, LANES - spin * width, 1)
        return carry

    lax.fori_loop(0, count // 2, spin_block, 0, unroll=few)

    def chunk(step, carry):
        for at in range(CHUNK):
            place = (step * CHUNK + at) * count * FACTOR

            def term(index, total):
                return total + turned[index] * spread[pl.ds(place + index, 1), :]

            gathered[:, at * LANES : (at + 1) * LANES] = lax.fori_loop(
                0, count * FACTOR, term, jnp.zeros((whole_y, LANES), jnp.float32), unroll=True if few else 4
            )
        values = dot(forward[...], tripled(gathered[...], 0))
        own = tables[:whole_y, :]
        total = jnp.concatenate(
            [own + tables[pl.ds(whole_y + step * CHUNK + at, 1), :] for at in range(CHUNK)], axis=1
        )
        scale = jnp.where(total > 0.0, 1.0 / jnp.where(total > 0.0, total, 1.0), 0.0)
        result = dot(inverse[...], tripled(values * scale, 0))
        for at in range(CHUNK):
            back[step * CHUNK + at] = result[:, at * LANES : (at + 1) * LANES]
        return carry

    lax.fori_loop(0, quads // CHUNK, chunk, 0)

    for group in range(groups):
        def collect(index, totals):
            whole = back[index]
            value, slope = whole[:fine], whole[fine:]
            along = own_tables[pl.ds(index * 2 * groups + group, 1), :]
            along_slope = own_tables[pl.ds((index * 2 + 1) * groups + group, 1), :]
            return (
                totals[0] + value * along_slope, totals[1] + slope * along, totals[2] + value * along,
            )

        zero = jnp.zeros((fine, LANES), jnp.float32)
        totals = lax.fori_loop(0, quads, collect, (zero, zero, zero), unroll=few)
        for component in range(3):
            columns[component, group * fine : (group + 1) * fine, :] = totals[component]
    for component in range(3):
        result = dot(tripled(columns[component], 1), back_z[1 if component == 2 else 0])
        for group in range(groups):
            force[component, group] = result[group * fine : (group + 1) * fine]


def along_first(columns, matrix, out_smooth, out_deriv, wide):
    rows, depth = matrix.shape[0] // 2, LANES
    for start in range(0, len(columns), CHUNK):
        some = columns[start : start + CHUNK]
        stacked = jnp.concatenate(
            [tripled(jnp.concatenate(parts(), axis=0), 0) for _, parts in some], axis=1
        )
        result = dot(matrix, stacked)
        for at, (col, _) in enumerate(some):
            out_smooth[pl.ds(col, rows, stride=wide), :] = result[:rows, at * depth : (at + 1) * depth]
            out_deriv[pl.ds(col, rows, stride=wide), :] = result[rows:, at * depth : (at + 1) * depth]


def along_others(smooth_x, deriv_x, rows, wide, along_y, smooth_z, deriv_z):
    pieces = [[], [], []]
    count, depth = along_y.shape[0] // 2, LANES
    for row in rows:
        values = jnp.concatenate(
            [smooth_x[row * wide : (row + 1) * wide, :], deriv_x[row * wide : (row + 1) * wide, :]], axis=1
        )
        result = dot(along_y, tripled(values, 0))
        for at, piece in enumerate((result[:count, depth:], result[count:, :depth], result[:count, :depth])):
            pieces[at].append(tripled(piece, 1))
    smooth = dot(jnp.concatenate(pieces[0] + pieces[1], axis=0), smooth_z)
    deriv = dot(jnp.concatenate(pieces[2], axis=0), deriv_z)
    number = len(rows)
    return [
        [smooth[at * count : (at + 1) * count] for at in range(number)],
        [smooth[(number + at) * count : (number + at + 1) * count] for at in range(number)],
        [deriv[at * count : (at + 1) * count] for at in range(number)],
    ]


def inner_kernel(
    own, swapped, crossed, bands, momenta_far, scale_row,
    spread_far, tables_far, own_tables_far, back_z_far, forward_far, inverse_far,
    partial, spread, tables, own_tables, back_z, forward, inverse,
    smooth_x, deriv_x, momenta, sem, loads, *, group, radius
):
    gx, gy = 2 * lax.axis_index("pair") + lax.axis_index("core"), lax.axis_index("gy")
    loading = [
        pltpu.make_async_copy(source, target, loads.at[at])
        for at, (source, target) in enumerate((
            (spread_far, spread), (tables_far, tables), (own_tables_far.at[gx], own_tables), (back_z_far, back_z),
            (forward_far, forward), (inverse_far.at[gy], inverse),
        ))
    ]
    arriving = pltpu.make_async_copy(momenta_far, momenta, sem)
    arriving.start()
    for copy in loading:
        copy.start()
    rows, cols, depth = own.shape
    places = band_rows(rows, cols, depth, radius)
    along_x, own_y, smooth_z, deriv_z = [band(bands, places, n) for n in ("x", "own", "smooth", "deriv")]
    along_first(
        [(col, lambda col=col: [own[:, col, :], swapped[:, col, :], crossed[:, col, :]]) for col in range(cols)],
        along_x, smooth_x, deriv_x, cols,
    )
    arriving.wait()
    scale = scale_row[0:1, :]
    for start in range(0, rows, group):
        short = along_others(
            smooth_x, deriv_x, range(start, start + group), cols, own_y, smooth_z, deriv_z
        )
        for component in range(3):
            for at in range(group):
                partial[component, start + at] = momenta[component, start + at] + scale * short[component][at]
    for copy in loading:
        copy.wait()


def outer_kernel(
    left, right, beside_left, beside_right, cross_left, cross_right, bands, partial, scale_row, force,
    kicked, smooth_x, deriv_x, staged, sems, *, group,
):
    radius = left.shape[0]
    _, rows, cols, depth = partial.shape
    places = band_rows(rows, cols, depth, radius)
    along_x, sides_y, smooth_z, deriv_z = [band(bands, places, n) for n in ("x", "sides", "smooth", "deriv")]
    along_first(
        [(col, lambda col=col: [left[col], beside_left[col], cross_left[col]]) for col in range(radius)]
        + [
            (radius + col, lambda col=col: [right[col], beside_right[col], cross_right[col]])
            for col in range(radius)
        ],
        along_x, smooth_x, deriv_x, 2 * radius,
    )
    scale = scale_row[0:1, :]
    copies = []
    for start in range(0, rows, group):
        short = along_others(
            smooth_x, deriv_x, range(start, start + group), 2 * radius, sides_y, smooth_z, deriv_z
        )
        for component in range(3):
            for at in range(group):
                row = start + at
                far = force[component, row // FACTOR]
                base = partial[component, row]
                near = short[component][at]
                staged[component, row, :radius] = base[:radius] + scale * (near[:radius] + far[:radius])
                staged[component, row, radius : cols - radius] = (
                    base[radius : cols - radius] + scale * far[radius : cols - radius]
                )
                staged[component, row, cols - radius :] = base[cols - radius :] + scale * (
                    near[radius:] + far[cols - radius :]
                )
        copy = pltpu.make_async_copy(
            staged.at[:, pl.ds(start, group)], kicked.at[:, pl.ds(start, group)], sems.at[start // group]
        )
        copy.start()
        copies.append(copy)
    for copy in copies:
        copy.wait()


def call(body, outs, n_in, scratch=(), smem=(), far=(), near=(), kept=False, spaces=None, mib=8, cost=10**6):
    made = pl.pallas_call(
        body,
        out_shape=[
            pltpu.VMEM(s, d) if (kept if isinstance(kept, bool) else kept[at]) else jax.ShapeDtypeStruct(s, d)
            for at, (s, d) in enumerate(outs)
        ],
        in_specs=[SMEM if at in smem else HBM if at in far else VMEM for at in range(n_in)],
        out_specs=spaces or [VMEM for _ in outs],
        scratch_shapes=list(scratch),
        cost_estimate=pl.CostEstimate(flops=cost, bytes_accessed=cost, transcendentals=0),
        compiler_params=pltpu.CompilerParams(vmem_limit_bytes=mib * 1024 * 1024),
    )

    def run(*operands):
        return made(*[
            pltpu.with_memory_space_constraint(o, pltpu.HBM) if at in far
            else pltpu.with_memory_space_constraint(o, pltpu.VMEM) if at in near else o
            for at, o in enumerate(operands)
        ])

    return run


def per_device(density, momenta, smooth_taps, deriv_taps, kick_step):
    rows, cols, depth = density.shape
    radius = (smooth_taps.shape[0] - 1) // 2
    count_gx, count_gy = 2 * lax.axis_size("pair"), lax.axis_size("gy")
    assert rows == radius and cols >= 2 * radius and depth == LANES
    groups, lines, deep = rows // FACTOR, cols // FACTOR, depth // FACTOR
    assert groups == FACTOR and groups * deep == LANES
    coarse_x, coarse_y = groups * count_gx, lines * count_gy
    quads = coarse_x // groups
    assert quads % CHUNK == 0
    padded = -(-lines // 8) * 8
    f, b = jnp.float32, jnp.bfloat16

    basis_x, waves_x = real_basis(coarse_x)
    basis_y, waves_y = real_basis(coarse_y)
    basis_z, waves_z = real_basis(deep)

    pool = split_table(np.tile(np.repeat(basis_z.T, FACTOR, 0) / FACTOR**3, (1, groups)), 0)
    own, head, tail, coarse = call(
        prepare_kernel,
        [((rows, cols, depth), f), ((radius, rows, depth), f), ((radius, rows, depth), f), ((count_gx // 2 * count_gy, padded, LANES), f)],
        2,
        [pltpu.VMEM(pool.shape, b), pltpu.VMEM((groups * cols, depth), f), DMA((groups + 1,))], far=(0, 1),
        kept=(True, True, True, count_gx <= CHUNK),
    )(density, jnp.asarray(pool))

    def shift(values, pairs):
        return lax.ppermute(values, ("pair", "core", "gy"), [
            (a * count_gy + c, d * count_gy + e) for (a, c), (d, e) in pairs
        ])

    every = [(i, j) for i in range(count_gx) for j in range(count_gy)]
    beside = lambda i: i + 1 if i % 2 == 0 else i - 1
    across = lambda i: (i - 1) % count_gx if i % 2 == 0 else (i + 1) % count_gx
    crossed = shift(density, [((i, j), (across(i), j)) for i, j in every])
    swapped = shift(density, [((i, j), (beside(i), j)) for i, j in every])
    left = shift(tail, [((i, j), (i, (j + 1) % count_gy)) for i, j in every])
    right = shift(head, [((i, j), (i, (j - 1) % count_gy)) for i, j in every])
    cross_left = shift(tail, [((i, j), (across(i), (j + 1) % count_gy)) for i, j in every])
    cross_right = shift(head, [((i, j), (across(i), (j - 1) % count_gy)) for i, j in every])

    blocks = lax.all_to_all(coarse, ("pair", "gy"), split_axis=0, concat_axis=0, tiled=True)
    beside_blocks = shift(blocks, [((i, j), (beside(i), j)) for i, j in every])

    places = band_rows(rows, cols, depth, radius)
    bands, scale = call(
        functools.partial(bands_kernel, rows=rows, cols=cols, depth=depth, radius=radius),
        [((max(p[1] for p in places.values()), max(p[2] for p in places.values())), b), ((8, LANES), f)],
        3, [pltpu.SMEM(smooth_taps.shape, f), pltpu.SMEM(deriv_taps.shape, f), DMA((2,))], far=(0, 1), smem=(2,), kept=True,
    )(smooth_taps, deriv_taps, kick_step)

    spread = np.zeros((quads, count_gx, groups, groups, deep))
    for turn in range(groups):
        for j in range(groups):
            for quad in range(quads):
                spread[quad, :, turn, j, :] = basis_x[quad * groups + j].reshape(count_gx, groups)[
                    :, (j + turn) % groups
                ][:, None]
    back_y = np.concatenate([
        np.repeat(t.T.reshape(count_gy, lines, coarse_y), FACTOR, 1) for t in (basis_y, centred(basis_y))
    ], 1)
    back_x = np.stack([basis_x, centred(basis_x)])
    back_x = back_x.reshape(2, quads, groups, count_gx, groups).transpose(3, 1, 0, 4, 2)
    back_x = np.repeat(back_x[..., None], deep, -1).reshape(count_gx, -1, LANES)
    back_z = np.stack([
        np.tile(np.repeat(t, FACTOR, 1), (groups, 1)) * LONG_COUPLING for t in (basis_z, centred(basis_z))
    ])
    other = (eigenvalues(waves_x, coarse_x).reshape(quads, groups, 1) + eigenvalues(waves_z, deep)).reshape(
        quads, LANES
    )
    second = np.repeat(eigenvalues(waves_y, coarse_y)[:, None], LANES, 1)
    far_tables = [
        spread.reshape(-1, LANES).astype(np.float32),
        np.concatenate([second, other]).astype(np.float32), back_x.astype(np.float32),
        split_table(back_z, 1), split_table(basis_y, 1), split_table(back_y, 2),
    ]

    beside_left = shift(left, [((i, j), (beside(i), j)) for i, j in every])
    beside_right = shift(right, [((i, j), (beside(i), j)) for i, j in every])
    near_tables = [(t.shape[1:] if at in (2, 5) else t.shape, t.dtype) for at, t in enumerate(far_tables)]
    far_tables = [jnp.asarray(t) for t in far_tables]
    partial, *near_tables = call(
        functools.partial(inner_kernel, group=GROUP, radius=radius),
        [((3, rows, cols, depth), f)] + near_tables, 12,
        [pltpu.VMEM((rows * cols, depth), f), pltpu.VMEM((rows * cols, depth), f),
         pltpu.VMEM((3, rows, cols, depth), f), DMA, DMA((6,))],
        far=(4, 6, 7, 8, 9, 10, 11), near=(0, 1, 2, 3, 5), kept=(True,) + (count_gx <= CHUNK,) * 6,
        mib=8 if count_gx <= CHUNK else 52,
    )(own, swapped, crossed, bands, momenta, scale, *far_tables)
    (force,) = call(
        functools.partial(solve_kernel, lines=lines),
        [((3, groups, cols, depth), f)], 8,
        [pltpu.VMEM((coarse_y, CHUNK * LANES), f), pltpu.VMEM((coarse_x, coarse_y, LANES), f),
           pltpu.VMEM((quads, 2 * cols, LANES), f), pltpu.VMEM((3, groups * cols, LANES), f)],
        near=tuple(range(8)) if count_gx <= CHUNK else (), kept=count_gx <= CHUNK,
        mib=10 if count_gx <= CHUNK else 52,
    )(blocks, beside_blocks, *near_tables)
    (kicked,) = call(
        functools.partial(outer_kernel, group=GROUP),
        [((3, rows, cols, depth), f)], 10,
        [pltpu.VMEM((rows * 2 * radius, depth), f), pltpu.VMEM((rows * 2 * radius, depth), f),
         pltpu.VMEM((3, rows, cols, depth), f), DMA((rows // GROUP,))],
        near=tuple(range(10)), spaces=[HBM], mib=8,
    )(left, right, beside_left, beside_right, cross_left, cross_right, bands, partial, scale, force)
    return kicked


def solution(mesh):
    assert mesh.shape["gx"] % 2 == 0
    count_gx, count_gy = mesh.shape["gx"], mesh.shape["gy"]
    mesh = jax.sharding.Mesh(
        np.asarray(mesh.devices).reshape(count_gx // 2, 2, count_gy), ("pair", "core", "gy")
    )

    gx = ("pair", "core")
    in_specs = (P(gx, "gy", None), P(None, gx, "gy", None), P(), P(), P())
    out_specs = P(None, gx, "gy", None)
    return jax.shard_map(per_device, mesh=mesh, in_specs=in_specs, out_specs=out_specs, check_vma=False)
```

```python
import functools
import math

import jax
import jax.numpy as jnp
import ml_dtypes
import numpy as np
from jax import lax
from jax.experimental import pallas as pl
from jax.experimental.pallas import tpu as pltpu
from jax.sharding import PartitionSpec as P


FACTOR = 4
LANES = 128
CHUNK = 8
GROUP = 16
SIDE_GROUP = 8
TILE = 4
LONG_COUPLING = 16.0
VMEM = pl.BlockSpec(memory_space=pltpu.VMEM)
SMEM = pl.BlockSpec(memory_space=pltpu.SMEM)
HBM = pl.BlockSpec(memory_space=pltpu.HBM)
DMA = pltpu.SemaphoreType.DMA


def real_basis(count):
    places = np.arange(count, dtype=np.float64)
    rows, waves = [np.full(count, 1.0 / math.sqrt(count))], [0]
    for wave in range(1, (count + 1) // 2):
        phase = 2.0 * math.pi * wave * places / count
        rows += [math.sqrt(2.0 / count) * np.cos(phase), math.sqrt(2.0 / count) * np.sin(phase)]
        waves += [wave, wave]
    if count % 2 == 0:
        rows.append(np.cos(math.pi * places) / math.sqrt(count))
        waves.append(count // 2)
    return np.stack(rows), np.array(waves)


def centred(basis):
    return 0.5 * (np.roll(basis, -1, 1) - np.roll(basis, 1, 1))


def eigenvalues(waves, count):
    return 2.0 - 2.0 * np.cos(2.0 * math.pi * waves / count)


def split_table(table, axis):
    table = np.asarray(table, dtype=np.float32)
    high = table.astype(ml_dtypes.bfloat16)
    low = (table - high.astype(np.float32)).astype(ml_dtypes.bfloat16)
    return np.concatenate([high, low, high], axis)


def split(values):
    high = values.astype(jnp.bfloat16)
    low = (values - high.astype(jnp.float32)).astype(jnp.bfloat16)
    return high, low


def tripled(values, axis):
    high, low = split(values)
    return jnp.concatenate([high, high, low], axis=axis)


def dot(left, right):
    return jnp.dot(left, right, preferred_element_type=jnp.float32)


def side_start(which, radius, cols):
    high = lax.axis_index("gy") % 2 == which
    return pl.multiple_of(jnp.where(high, cols - radius, 0), 16)


def prepare_kernel(
    density_far, pool_far, smooth_far, deriv_far, density, bands, strip_a_far, strip_b_far, coarse_far,
    coarse, pool_table, pooled, smooth, deriv, sems,
):
    rows, cols, depth = density.shape
    radius = strip_a_far.shape[1]
    groups, lines = rows // FACTOR, cols // FACTOR
    step = FACTOR
    copies = [
        pltpu.make_async_copy(
            density_far.at[pl.ds(step * group, step)], density.at[pl.ds(step * group, step)], sems.at[group]
        )
        for group in range(groups)
    ]
    for source, target in ((pool_far, pool_table), (smooth_far, smooth), (deriv_far, deriv)):
        copies.append(pltpu.make_async_copy(source, target, sems.at[len(copies)]))
    for copy in copies:
        copy.start()
    for group in range(groups):
        copies[group].wait()
        total = density[FACTOR * group]
        for at in range(1, FACTOR):
            total = total + density[FACTOR * group + at]
        pooled[group * cols : (group + 1) * cols, :] = total
    leaving = [
        pltpu.make_async_copy(
            density.at[:, pl.ds(side_start(which, radius, cols), radius)], target, sems.at[len(copies) + which]
        )
        for which, target in enumerate((strip_a_far, strip_b_far))
    ]
    for copy in leaving:
        copy.start()
    parts = []
    for group in range(groups):
        total = pooled[pl.ds(group * cols, lines, stride=FACTOR), :]
        for at in range(1, FACTOR):
            total = total + pooled[pl.ds(group * cols + at, lines, stride=FACTOR), :]
        parts.append(total)
    copies[groups].wait()
    waves = dot(tripled(jnp.concatenate(parts, axis=0), 1), pool_table[...])
    lane_group = lax.broadcasted_iota(jnp.int32, (lines, LANES), 1) // (LANES // groups)
    result = waves[:lines]
    for group in range(1, groups):
        result = jnp.where(lane_group == group, waves[group * lines : (group + 1) * lines], result)
    tiles = lines // TILE

    def spread_out(copy, carry):
        for tile in range(tiles):
            coarse[copy * tiles + tile] = result[tile * TILE : (tile + 1) * TILE]
        return carry

    lax.fori_loop(0, coarse.shape[0] // tiles, spread_out, 0, unroll=coarse.shape[0] <= 64)
    leaving.append(pltpu.make_async_copy(coarse, coarse_far, sems.at[len(copies) + 2]))
    leaving[-1].start()
    for copy in copies[groups + 1 :]:
        copy.wait()
    write_bands(smooth, deriv, bands, rows, cols, depth, radius)
    for copy in leaving:
        copy.wait()


def band_rows(rows, cols, depth, radius):
    sizes = {"x": (2 * rows, 3 * rows), "own": (2 * cols, cols), "smooth": (depth, depth), "deriv": (depth, depth)}
    sizes["sides"] = (4 * radius, 2 * radius)
    places, start = {}, 0
    for name, (height, width) in sizes.items():
        places[name] = (start, height, width)
        start += 2 * height
    return places, start


def band(bands, places, name):
    start, height, width = places[name]
    high = bands[start : start + height, :width]
    low = bands[start + height : start + 2 * height, :width]
    return jnp.concatenate([high, low, high], axis=0 if name in ("smooth", "deriv") else 1)


def write_bands(smooth, deriv, bands, rows, cols, depth, radius):
    taps = 2 * radius + 1
    odd = lax.axis_index("core")
    places, _ = band_rows(rows, cols, depth, radius)
    lane8 = lax.broadcasted_iota(jnp.int32, (8, LANES), 1)
    pair, turned_pair = [], []
    for weights in (smooth, deriv):
        row = turned = jnp.zeros((8, LANES), jnp.float32)
        for tap in range(taps):
            row = jnp.where(lane8 == tap, weights[tap], row)
            turned = jnp.where(lane8 == (LANES - tap) % LANES, weights[tap], turned)
        pair.append(row)
        turned_pair.append(turned)

    def toeplitz(row, height, shift):
        tall = jnp.concatenate([row] * (height // 8), axis=0)
        return pltpu.roll(tall, shift % LANES, 1, stride=1, stride_axis=0)

    def lanes_of(height):
        return lax.broadcasted_iota(jnp.int32, (height, LANES), 1)

    def write(name, matrix):
        high, low = split(matrix)
        start, height, _ = places[name]
        bands[start : start + height, :] = high
        bands[start + height : start + 2 * height, :] = low

    lane = lanes_of(rows)
    parts = []
    for row in pair:
        near = toeplitz(row, rows, -radius)
        later = jnp.where(lane < 2 * rows, near, toeplitz(row, rows, 2 * rows))
        earlier = jnp.where(
            lane < rows, near, jnp.where(lane < 2 * rows, toeplitz(row, rows, rows), toeplitz(row, rows, 0))
        )
        parts.append(jnp.where(odd == 1, earlier, later))
    write("x", jnp.concatenate(parts, axis=0))
    write("own", jnp.concatenate([toeplitz(row, cols, -radius) for row in pair], axis=0))
    lane, even = lanes_of(radius), lax.axis_index("gy") % 2 == 0
    parts = []
    for row in pair:
        nearer = jnp.where(even, toeplitz(row, radius, -2 * radius), toeplitz(row, radius, 0))
        other = jnp.where(even, toeplitz(row, radius, radius), toeplitz(row, radius, -radius))
        parts += [jnp.where(lane < radius, nearer, 0.0), jnp.where(lane < radius, 0.0, other)]
    write("sides", jnp.concatenate(parts, axis=0))
    for name, turned in zip(("smooth", "deriv"), turned_pair):
        write(name, toeplitz(turned, depth, radius))


def solve_kernel(
    blocks, beside_blocks, spread, tables, own_tables, back_z, forward, inverse, partial, scale_row, base,
    gathered, turned, back, columns, *, lines,
):
    core = lax.axis_index("core")
    rows, fine = partial.shape[1:3]
    groups = rows // FACTOR
    quads = back.shape[0]
    whole_y = gathered.shape[0]
    parts = whole_y // lines
    tiles = lines // TILE
    count = 2 * blocks.shape[0] // (parts * tiles)
    width = LANES // FACTOR
    few = count <= CHUNK

    def spin_block(pair, carry):
        for side, source in enumerate((blocks, beside_blocks)):
            for tile in range(parts * tiles):
                gathered[tile * TILE : (tile + 1) * TILE, :LANES] = source[pair * parts * tiles + tile]
            values = gathered[:, :LANES]
            place = (2 * pair + (core if side == 0 else 1 - core)) * FACTOR
            for spin in range(FACTOR):
                turned[place + spin] = values if spin == 0 else pltpu.roll(values, LANES - spin * width, 1)
        return carry

    lax.fori_loop(0, count // 2, spin_block, 0, unroll=few)

    def chunk(step, carry):
        for at in range(CHUNK):
            place = (step * CHUNK + at) * count * FACTOR

            def term(index, total):
                return total + turned[index] * spread[pl.ds(place + index, 1), :]

            gathered[:, at * LANES : (at + 1) * LANES] = lax.fori_loop(
                0, count * FACTOR, term, jnp.zeros((whole_y, LANES), jnp.float32), unroll=True if few else 4
            )
        values = dot(forward[...], tripled(gathered[...], 0))
        own = tables[:whole_y, :]
        total = jnp.concatenate(
            [own + tables[pl.ds(whole_y + step * CHUNK + at, 1), :] for at in range(CHUNK)], axis=1
        )
        scale = jnp.where(total > 0.0, 1.0 / jnp.where(total > 0.0, total, 1.0), 0.0)
        result = dot(inverse[...], tripled(values * scale, 0))
        for at in range(CHUNK):
            back[step * CHUNK + at] = result[:, at * LANES : (at + 1) * LANES]
        return carry

    lax.fori_loop(0, quads // CHUNK, chunk, 0)

    for group in range(groups):
        def collect(index, totals):
            whole = back[index]
            value, slope = whole[:fine], whole[fine:]
            along = own_tables[pl.ds(index * 2 * groups + group, 1), :]
            along_slope = own_tables[pl.ds((index * 2 + 1) * groups + group, 1), :]
            return (
                totals[0] + value * along_slope, totals[1] + slope * along, totals[2] + value * along,
            )

        zero = jnp.zeros((fine, LANES), jnp.float32)
        totals = lax.fori_loop(0, quads, collect, (zero, zero, zero), unroll=few)
        for component in range(3):
            columns[component, group * fine : (group + 1) * fine, :] = totals[component]
    for component in range(3):
        columns[component] = dot(tripled(columns[component], 1), back_z[1 if component == 2 else 0])
    scale = scale_row[0:1, :]
    for component in range(3):
        for row in range(rows):
            group = row // FACTOR
            far = columns[component, group * fine : (group + 1) * fine, :]
            base[component, row] = partial[component, row] + scale * far


def along_first(columns, matrix, smooth_x, deriv_x):
    rows, depth = matrix.shape[0] // 2, LANES
    for start in range(0, len(columns), CHUNK):
        some = columns[start : start + CHUNK]
        stacked = jnp.concatenate([tripled(jnp.concatenate(parts(), axis=0), 0) for parts in some], axis=1)
        result = dot(matrix, stacked)
        for at in range(len(some)):
            place = (start + at) * rows
            smooth_x[place : place + rows, :] = result[:rows, at * depth : (at + 1) * depth]
            deriv_x[place : place + rows, :] = result[rows:, at * depth : (at + 1) * depth]


def along_others(smooth_x, deriv_x, some, rows, wide, along_y, smooth_z, deriv_z):
    pieces = [[], [], []]
    count, depth = along_y.shape[0] // 2, LANES
    for row in some:
        values = jnp.concatenate([x[pl.ds(row, wide, stride=rows), :] for x in (smooth_x, deriv_x)], axis=1)
        result = dot(along_y, tripled(values, 0))
        for at, piece in enumerate((result[:count, depth:], result[count:, :depth], result[:count, :depth])):
            pieces[at].append(tripled(piece, 1))
    smooth = dot(jnp.concatenate(pieces[0] + pieces[1], axis=0), smooth_z)
    deriv = dot(jnp.concatenate(pieces[2], axis=0), deriv_z)
    number = len(some)
    return [
        [smooth[at * count : (at + 1) * count] for at in range(number)],
        [smooth[(number + at) * count : (number + at + 1) * count] for at in range(number)],
        [deriv[at * count : (at + 1) * count] for at in range(number)],
    ]


def load_kernel(
    spread_far, tables_far, own_tables_far, back_z_far, forward_far, inverse_far,
    spread, tables, own_tables, back_z, forward, inverse, sems,
):
    gx, gy = 2 * lax.axis_index("pair") + lax.axis_index("core"), lax.axis_index("gy")
    copies = [
        pltpu.make_async_copy(source, target, sems.at[at])
        for at, (source, target) in enumerate((
            (spread_far, spread), (tables_far, tables), (own_tables_far.at[gx], own_tables), (back_z_far, back_z),
            (forward_far, forward), (inverse_far.at[gy], inverse),
        ))
    ]
    for copy in copies:
        copy.start()
    for copy in copies:
        copy.wait()


def inner_kernel(
    own, swapped, crossed, bands, scale_row, momenta_far, partial, smooth_x, deriv_x, momenta, sems, *, group, radius
):
    _, rows, cols, depth = partial.shape
    arriving = [
        pltpu.make_async_copy(momenta_far.at[component], momenta.at[component], sems.at[component])
        for component in range(3)
    ]
    for copy in arriving:
        copy.start()
    places, _ = band_rows(rows, cols, depth, radius)
    along_x, own_y, smooth_z, deriv_z = [band(bands, places, n) for n in ("x", "own", "smooth", "deriv")]
    along_first(
        [lambda col=col: [x[pl.ds(col, rows, stride=cols), :] for x in (own, swapped, crossed)] for col in range(cols)],
        along_x, smooth_x, deriv_x,
    )
    for start in range(0, rows, group):
        short = along_others(
            smooth_x, deriv_x, range(start, start + group), rows, cols, own_y, smooth_z, deriv_z
        )
        for component in range(3):
            for at in range(group):
                partial[component, start + at] = short[component][at]
    scale = scale_row[0:1, :]
    for component in range(3):
        arriving[component].wait()
        for row in range(rows):
            partial[component, row] = momenta[component, row] + scale * partial[component, row]


def cut_kernel(tile, strip):
    radius = strip.shape[1]
    strip[...] = tile[:, pl.ds(side_start(1, radius, tile.shape[1]), radius), :]


def outer_kernel(
    strip_a, strip_b, beside_a, beside_b, cross_a, cross_b, bands, scale_row, base, kicked,
    smooth_x, deriv_x, staged, sems, *, group,
):
    _, rows, cols, depth = base.shape
    radius = strip_a.shape[0] // rows
    places, _ = band_rows(rows, cols, depth, radius)
    along_x, along_y, smooth_z, deriv_z = [band(bands, places, n) for n in ("x", "sides", "smooth", "deriv")]
    along_first(
        [
            lambda col=col, blocks=blocks: [x[pl.ds(col, rows, stride=radius), :] for x in blocks]
            for blocks in ((strip_a, beside_a, cross_a), (strip_b, beside_b, cross_b)) for col in range(radius)
        ],
        along_x, smooth_x, deriv_x,
    )
    scale = scale_row[0:1, :]
    copies = []
    for start in range(0, rows, group):
        short = along_others(
            smooth_x, deriv_x, range(start, start + group), rows, 2 * radius, along_y, smooth_z, deriv_z
        )
        for component in range(3):
            for at in range(group):
                row = start + at
                staged[component, row, radius : cols - radius] = base[component, row, radius : cols - radius]
                for which in range(2):
                    side = pl.ds(side_start(which, radius, cols), radius)
                    near = short[component][at][which * radius : (which + 1) * radius]
                    staged[component, row, side] = base[component, row, side] + scale * near
        copies.append(pltpu.make_async_copy(
            staged.at[:, pl.ds(start, group)], kicked.at[:, pl.ds(start, group)], sems.at[start // group]
        ))
        copies[-1].start()
    for copy in copies:
        copy.wait()


def call(body, outs, n_in, scratch=(), smem=(), far=(), near=(), kept=False, spaces=None, mib=8, cost=10**6, alias={}):
    made = pl.pallas_call(
        body,
        out_shape=[
            pltpu.VMEM(s, d) if (kept if isinstance(kept, bool) else kept[at]) else jax.ShapeDtypeStruct(s, d)
            for at, (s, d) in enumerate(outs)
        ],
        in_specs=[SMEM if at in smem else HBM if at in far else VMEM for at in range(n_in)],
        out_specs=spaces or [VMEM for _ in outs],
        scratch_shapes=list(scratch),
        input_output_aliases=alias,
        cost_estimate=pl.CostEstimate(flops=cost, bytes_accessed=cost, transcendentals=0),
        compiler_params=pltpu.CompilerParams(vmem_limit_bytes=mib * 1024 * 1024),
    )

    def run(*operands):
        return made(*[
            pltpu.with_memory_space_constraint(o, pltpu.HBM) if at in far
            else pltpu.with_memory_space_constraint(o, pltpu.VMEM) if at in near else o
            for at, o in enumerate(operands)
        ])

    return run


def per_device(density, momenta, smooth_taps, deriv_taps, kick_step):
    rows, cols, depth = density.shape
    radius = (smooth_taps.shape[0] - 1) // 2
    count_gx, count_gy = 2 * lax.axis_size("pair"), lax.axis_size("gy")
    assert count_gy % 2 == 0 and radius % 16 == 0
    assert rows == radius and cols >= 2 * radius and depth == LANES
    groups, lines, deep = rows // FACTOR, cols // FACTOR, depth // FACTOR
    assert groups == FACTOR and groups * deep == LANES
    coarse_x, coarse_y = groups * count_gx, lines * count_gy
    quads = coarse_x // groups
    assert quads % CHUNK == 0
    assert lines % TILE == 0
    f, b = jnp.float32, jnp.bfloat16

    basis_x, waves_x = real_basis(coarse_x)
    basis_y, waves_y = real_basis(coarse_y)
    basis_z, waves_z = real_basis(deep)

    pool = split_table(np.tile(np.repeat(basis_z.T, FACTOR, 0) / FACTOR**3, (1, groups)), 0)
    _, band_height = band_rows(rows, cols, depth, radius)
    own, bands, send_a, send_b, coarse = call(
        prepare_kernel,
        [((rows, cols, depth), f), ((band_height, LANES), b), ((rows, radius, depth), f), ((rows, radius, depth), f),
         ((count_gx // 2 * count_gy * (lines // TILE), TILE, LANES), f)],
        4,
        [pltpu.VMEM((count_gx // 2 * count_gy * (lines // TILE), TILE, LANES), f), pltpu.VMEM(pool.shape, b),
         pltpu.VMEM((groups * cols, depth), f), pltpu.SMEM(smooth_taps.shape, f), pltpu.SMEM(deriv_taps.shape, f),
         DMA((groups + 6,))],
        far=(0, 1, 2, 3), kept=(True, True, False, False, False), spaces=[VMEM, VMEM, HBM, HBM, HBM],
        mib=8 if count_gx <= CHUNK else 24,
    )(density, jnp.asarray(pool), smooth_taps, deriv_taps)

    def shift(values, pairs):
        return lax.ppermute(values, ("pair", "core", "gy"), [
            (a * count_gy + c, d * count_gy + e) for (a, c), (d, e) in pairs
        ])

    every = [(i, j) for i in range(count_gx) for j in range(count_gy)]
    beside = lambda i: i + 1 if i % 2 == 0 else i - 1
    across = lambda i: (i - 1) % count_gx if i % 2 == 0 else (i + 1) % count_gx
    crossed = shift(density, [((i, j), (across(i), j)) for i, j in every])
    swapped = shift(density, [((i, j), (beside(i), j)) for i, j in every])
    pair_a = lambda j: j + 1 if j % 2 == 0 else j - 1
    pair_b = lambda j: (j + 1) % count_gy if j % 2 == 1 else (j - 1) % count_gy
    strip_a = shift(send_a, [((i, j), (i, pair_a(j))) for i, j in every])
    strip_b = shift(send_b, [((i, j), (i, pair_b(j))) for i, j in every])
    cross_a = shift(strip_a, [((i, j), (across(i), j)) for i, j in every])
    (crossed_b,) = call(cut_kernel, [((rows, radius, depth), f)], 1, near=(0,), kept=True)(crossed)
    cross_b = shift(crossed_b, [((i, j), (i, pair_b(j))) for i, j in every])

    blocks = lax.all_to_all(coarse, ("pair", "gy"), split_axis=0, concat_axis=0, tiled=True)
    beside_blocks = shift(blocks, [((i, j), (beside(i), j)) for i, j in every])

    scale = jnp.broadcast_to(kick_step, (8, LANES))
    spread = np.zeros((quads, count_gx, groups, groups, deep))
    for turn in range(groups):
        for j in range(groups):
            for quad in range(quads):
                spread[quad, :, turn, j, :] = basis_x[quad * groups + j].reshape(count_gx, groups)[
                    :, (j + turn) % groups
                ][:, None]
    back_y = np.concatenate([
        np.repeat(t.T.reshape(count_gy, lines, coarse_y), FACTOR, 1) for t in (basis_y, centred(basis_y))
    ], 1)
    back_x = np.stack([basis_x, centred(basis_x)])
    back_x = back_x.reshape(2, quads, groups, count_gx, groups).transpose(3, 1, 0, 4, 2)
    back_x = np.repeat(back_x[..., None], deep, -1).reshape(count_gx, -1, LANES)
    back_z = np.stack([
        np.tile(np.repeat(t, FACTOR, 1), (groups, 1)) * LONG_COUPLING for t in (basis_z, centred(basis_z))
    ])
    other = (eigenvalues(waves_x, coarse_x).reshape(quads, groups, 1) + eigenvalues(waves_z, deep)).reshape(
        quads, LANES
    )
    second = np.repeat(eigenvalues(waves_y, coarse_y)[:, None], LANES, 1)
    far_tables = [
        spread.reshape(-1, LANES).astype(np.float32),
        np.concatenate([second, other]).astype(np.float32), back_x.astype(np.float32),
        split_table(back_z, 1), split_table(basis_y, 1), split_table(back_y, 2),
    ]

    beside_a = shift(strip_a, [((i, j), (beside(i), j)) for i, j in every])
    beside_b = shift(strip_b, [((i, j), (beside(i), j)) for i, j in every])
    near_tables = [(t.shape[1:] if at in (2, 5) else t.shape, t.dtype) for at, t in enumerate(far_tables)]
    far_tables = [jnp.asarray(t) for t in far_tables]
    small = count_gx <= CHUNK
    near_tables = call(
        load_kernel, near_tables, 6, [DMA((6,))], far=tuple(range(6)), kept=small, mib=8 if small else 52,
    )(*far_tables)
    (partial,) = call(
        functools.partial(inner_kernel, group=GROUP, radius=radius),
        [((3, rows, cols, depth), f)], 6,
        [pltpu.VMEM((rows * cols, depth), f), pltpu.VMEM((rows * cols, depth), f),
         pltpu.VMEM((3, rows, cols, depth), f), DMA((3,))],
        far=(5,), near=(0, 1, 2, 3, 4), kept=True,
    )(*[x.reshape(rows * cols, depth) for x in (own, swapped, crossed)], bands, scale, momenta)
    (base,) = call(
        functools.partial(solve_kernel, lines=lines),
        [((3, rows, cols, depth), f)], 10,
        [pltpu.VMEM((coarse_y, CHUNK * LANES), f), pltpu.VMEM((coarse_x, coarse_y, LANES), f),
         pltpu.VMEM((quads, 2 * cols, LANES), f), pltpu.VMEM((3, groups * cols, LANES), f)],
        near=tuple(range(10)) if small else (), kept=small, mib=8 if small else 52, alias={8: 0},
    )(blocks, beside_blocks, *near_tables, partial, scale)
    strips = [x.reshape(rows * radius, depth) for x in (strip_a, strip_b, beside_a, beside_b, cross_a, cross_b)]
    (kicked,) = call(
        functools.partial(outer_kernel, group=SIDE_GROUP), [((3, rows, cols, depth), f)], 9,
        [pltpu.VMEM((2 * rows * radius, depth), f), pltpu.VMEM((2 * rows * radius, depth), f),
         pltpu.VMEM((3, rows, cols, depth), f), DMA((rows // SIDE_GROUP,))],
        near=tuple(range(9)), spaces=[HBM],
    )(*strips, bands, scale, base)
    return kicked


def solution(mesh):
    assert mesh.shape["gx"] % 2 == 0
    count_gx, count_gy = mesh.shape["gx"], mesh.shape["gy"]
    mesh = jax.sharding.Mesh(
        np.asarray(mesh.devices).reshape(count_gx // 2, 2, count_gy), ("pair", "core", "gy")
    )

    gx = ("pair", "core")
    in_specs = (P(gx, "gy", None), P(None, gx, "gy", None), P(), P(), P())
    out_specs = P(None, gx, "gy", None)
    return jax.shard_map(per_device, mesh=mesh, in_specs=in_specs, out_specs=out_specs, check_vma=False)
```

```python
import functools
import math

import jax
import jax.numpy as jnp
import ml_dtypes
import numpy as np
from jax import lax
from jax.experimental import pallas as pl
from jax.experimental.pallas import tpu as pltpu
from jax.sharding import PartitionSpec as P


FACTOR = 4
LANES = 128
CHUNK = 8
GROUP = 16
SIDE_GROUP = 8
TILE = 4
LONG_COUPLING = 16.0
VMEM = pl.BlockSpec(memory_space=pltpu.VMEM)
SMEM = pl.BlockSpec(memory_space=pltpu.SMEM)
HBM = pl.BlockSpec(memory_space=pltpu.HBM)
DMA = pltpu.SemaphoreType.DMA


def real_basis(count):
    places = np.arange(count, dtype=np.float64)
    rows, waves = [np.full(count, 1.0 / math.sqrt(count))], [0]
    for wave in range(1, (count + 1) // 2):
        phase = 2.0 * math.pi * wave * places / count
        rows += [math.sqrt(2.0 / count) * np.cos(phase), math.sqrt(2.0 / count) * np.sin(phase)]
        waves += [wave, wave]
    if count % 2 == 0:
        rows.append(np.cos(math.pi * places) / math.sqrt(count))
        waves.append(count // 2)
    return np.stack(rows), np.array(waves)


def centred(basis):
    return 0.5 * (np.roll(basis, -1, 1) - np.roll(basis, 1, 1))


def eigenvalues(waves, count):
    return 2.0 - 2.0 * np.cos(2.0 * math.pi * waves / count)


def split_table(table, axis):
    table = np.asarray(table, dtype=np.float32)
    high = table.astype(ml_dtypes.bfloat16)
    low = (table - high.astype(np.float32)).astype(ml_dtypes.bfloat16)
    return np.concatenate([high, low, high], axis)


def split(values):
    high = values.astype(jnp.bfloat16)
    low = (values - high.astype(jnp.float32)).astype(jnp.bfloat16)
    return high, low


def tripled(values, axis):
    high, low = split(values)
    return jnp.concatenate([high, high, low], axis=axis)


def dot(left, right):
    return jnp.dot(left, right, preferred_element_type=jnp.float32)


def side_start(which, radius, cols):
    high = lax.axis_index("gy") % 2 == which
    return pl.multiple_of(jnp.where(high, cols - radius, 0), 16)


def prepare_kernel(
    density_far, pool_far, smooth_far, deriv_far, density, bands, strip_a_far, strip_b_far, coarse_far,
    coarse, pool_table, pooled, smooth, deriv, sems,
):
    rows, cols, depth = density.shape
    radius = strip_a_far.shape[1]
    groups, lines = rows // FACTOR, cols // FACTOR
    step = FACTOR
    copies = [
        pltpu.make_async_copy(
            density_far.at[pl.ds(step * group, step)], density.at[pl.ds(step * group, step)], sems.at[group]
        )
        for group in range(groups)
    ]
    for source, target in ((pool_far, pool_table), (smooth_far, smooth), (deriv_far, deriv)):
        copies.append(pltpu.make_async_copy(source, target, sems.at[len(copies)]))
    for copy in copies:
        copy.start()
    for group in range(groups):
        copies[group].wait()
        total = density[FACTOR * group]
        for at in range(1, FACTOR):
            total = total + density[FACTOR * group + at]
        pooled[group * cols : (group + 1) * cols, :] = total
    leaving = [
        pltpu.make_async_copy(
            density.at[:, pl.ds(side_start(which, radius, cols), radius)], target, sems.at[len(copies) + which]
        )
        for which, target in enumerate((strip_a_far, strip_b_far))
    ]
    for copy in leaving:
        copy.start()
    parts = []
    for group in range(groups):
        total = pooled[pl.ds(group * cols, lines, stride=FACTOR), :]
        for at in range(1, FACTOR):
            total = total + pooled[pl.ds(group * cols + at, lines, stride=FACTOR), :]
        parts.append(total)
    copies[groups].wait()
    waves = dot(tripled(jnp.concatenate(parts, axis=0), 1), pool_table[...])
    lane_group = lax.broadcasted_iota(jnp.int32, (lines, LANES), 1) // (LANES // groups)
    result = waves[:lines]
    for group in range(1, groups):
        result = jnp.where(lane_group == group, waves[group * lines : (group + 1) * lines], result)
    tiles = lines // TILE

    def spread_out(copy, carry):
        for tile in range(tiles):
            coarse[copy * tiles + tile] = result[tile * TILE : (tile + 1) * TILE]
        return carry

    lax.fori_loop(0, coarse.shape[0] // tiles, spread_out, 0, unroll=coarse.shape[0] <= 64)
    leaving.append(pltpu.make_async_copy(coarse, coarse_far, sems.at[len(copies) + 2]))
    leaving[-1].start()
    for copy in copies[groups + 1 :]:
        copy.wait()
    write_bands(smooth, deriv, bands, rows, cols, depth, radius)
    for copy in leaving:
        copy.wait()


def band_rows(rows, cols, depth, radius):
    sizes = {"x": (2 * rows, 3 * rows), "own": (2 * cols, cols), "smooth": (depth, depth), "deriv": (depth, depth)}
    sizes["sides"] = (4 * radius, 2 * radius)
    places, start = {}, 0
    for name, (height, width) in sizes.items():
        places[name] = (start, height, width)
        start += 2 * height
    return places, start


def band(bands, places, name):
    start, height, width = places[name]
    high = bands[start : start + height, :width]
    low = bands[start + height : start + 2 * height, :width]
    return jnp.concatenate([high, low, high], axis=0 if name in ("smooth", "deriv") else 1)


def write_bands(smooth, deriv, bands, rows, cols, depth, radius):
    taps = 2 * radius + 1
    odd = lax.axis_index("core")
    places, _ = band_rows(rows, cols, depth, radius)
    lane8 = lax.broadcasted_iota(jnp.int32, (8, LANES), 1)
    pair, turned_pair = [], []
    for weights in (smooth, deriv):
        row = turned = jnp.zeros((8, LANES), jnp.float32)
        for tap in range(taps):
            row = jnp.where(lane8 == tap, weights[tap], row)
            turned = jnp.where(lane8 == (LANES - tap) % LANES, weights[tap], turned)
        pair.append(row)
        turned_pair.append(turned)

    def toeplitz(row, height, shift):
        tall = jnp.concatenate([row] * (height // 8), axis=0)
        return pltpu.roll(tall, shift % LANES, 1, stride=1, stride_axis=0)

    def lanes_of(height):
        return lax.broadcasted_iota(jnp.int32, (height, LANES), 1)

    def write(name, matrix):
        high, low = split(matrix)
        start, height, _ = places[name]
        bands[start : start + height, :] = high
        bands[start + height : start + 2 * height, :] = low

    lane = lanes_of(rows)
    parts = []
    for row in pair:
        near = toeplitz(row, rows, -radius)
        later = jnp.where(lane < 2 * rows, near, toeplitz(row, rows, 2 * rows))
        earlier = jnp.where(
            lane < rows, near, jnp.where(lane < 2 * rows, toeplitz(row, rows, rows), toeplitz(row, rows, 0))
        )
        parts.append(jnp.where(odd == 1, earlier, later))
    write("x", jnp.concatenate(parts, axis=0))
    write("own", jnp.concatenate([toeplitz(row, cols, -radius) for row in pair], axis=0))
    lane, even = lanes_of(radius), lax.axis_index("gy") % 2 == 0
    parts = []
    for row in pair:
        nearer = jnp.where(even, toeplitz(row, radius, -2 * radius), toeplitz(row, radius, 0))
        other = jnp.where(even, toeplitz(row, radius, radius), toeplitz(row, radius, -radius))
        parts += [jnp.where(lane < radius, nearer, 0.0), jnp.where(lane < radius, 0.0, other)]
    write("sides", jnp.concatenate(parts, axis=0))
    for name, turned in zip(("smooth", "deriv"), turned_pair):
        write(name, toeplitz(turned, depth, radius))


def solve_kernel(
    blocks, beside_blocks, spread, tables, own_tables, back_z, forward, inverse, partial, scale_row, base,
    gathered, turned, back, columns, *, lines,
):
    core = lax.axis_index("core")
    rows, fine = partial.shape[1:3]
    groups = rows // FACTOR
    quads = back.shape[0]
    whole_y = gathered.shape[0]
    parts = whole_y // lines
    tiles = lines // TILE
    count = 2 * blocks.shape[0] // (parts * tiles)
    width = LANES // FACTOR
    few = count <= CHUNK

    def spin_block(pair, carry):
        for side, source in enumerate((blocks, beside_blocks)):
            for tile in range(parts * tiles):
                gathered[tile * TILE : (tile + 1) * TILE, :LANES] = source[pair * parts * tiles + tile]
            values = gathered[:, :LANES]
            place = (2 * pair + (core if side == 0 else 1 - core)) * FACTOR
            for spin in range(FACTOR):
                turned[place + spin] = values if spin == 0 else pltpu.roll(values, LANES - spin * width, 1)
        return carry

    lax.fori_loop(0, count // 2, spin_block, 0, unroll=few)

    def chunk(step, carry):
        for at in range(CHUNK):
            place = (step * CHUNK + at) * count * FACTOR

            def term(index, total):
                return total + turned[index] * spread[pl.ds(place + index, 1), :]

            gathered[:, at * LANES : (at + 1) * LANES] = lax.fori_loop(
                0, count * FACTOR, term, jnp.zeros((whole_y, LANES), jnp.float32), unroll=True if few else 4
            )
        values = dot(forward[...], tripled(gathered[...], 0))
        own = tables[:whole_y, :]
        total = jnp.concatenate(
            [own + tables[pl.ds(whole_y + step * CHUNK + at, 1), :] for at in range(CHUNK)], axis=1
        )
        scale = jnp.where(total > 0.0, 1.0 / jnp.where(total > 0.0, total, 1.0), 0.0)
        result = dot(inverse[...], tripled(values * scale, 0))
        for at in range(CHUNK):
            back[step * CHUNK + at] = result[:, at * LANES : (at + 1) * LANES]
        return carry

    lax.fori_loop(0, quads // CHUNK, chunk, 0)

    for group in range(groups):
        def collect(index, totals):
            whole = back[index]
            value, slope = whole[:fine], whole[fine:]
            along = own_tables[pl.ds(index * 2 * groups + group, 1), :]
            along_slope = own_tables[pl.ds((index * 2 + 1) * groups + group, 1), :]
            return (
                totals[0] + value * along_slope, totals[1] + slope * along, totals[2] + value * along,
            )

        zero = jnp.zeros((fine, LANES), jnp.float32)
        totals = lax.fori_loop(0, quads, collect, (zero, zero, zero), unroll=few)
        for component in range(3):
            columns[component, group * fine : (group + 1) * fine, :] = totals[component]
    for component in range(3):
        columns[component] = dot(tripled(columns[component], 1), back_z[1 if component == 2 else 0])
    scale = scale_row[0:1, :]
    for component in range(3):
        for row in range(rows):
            group = row // FACTOR
            far = columns[component, group * fine : (group + 1) * fine, :]
            base[component, row] = partial[component, row] + scale * far


def along_first(columns, matrix, smooth_x, deriv_x):
    rows, depth = matrix.shape[0] // 2, LANES
    for start in range(0, len(columns), CHUNK):
        some = columns[start : start + CHUNK]
        stacked = jnp.concatenate([tripled(jnp.concatenate(parts(), axis=0), 0) for parts in some], axis=1)
        result = dot(matrix, stacked)
        for at in range(len(some)):
            place = (start + at) * rows
            smooth_x[place : place + rows, :] = result[:rows, at * depth : (at + 1) * depth]
            deriv_x[place : place + rows, :] = result[rows:, at * depth : (at + 1) * depth]


def along_others(smooth_x, deriv_x, some, rows, wide, along_y, smooth_z, deriv_z):
    pieces = [[], [], []]
    count, depth = along_y.shape[0] // 2, LANES
    for row in some:
        values = jnp.concatenate([x[pl.ds(row, wide, stride=rows), :] for x in (smooth_x, deriv_x)], axis=1)
        result = dot(along_y, tripled(values, 0))
        for at, piece in enumerate((result[:count, depth:], result[count:, :depth], result[:count, :depth])):
            pieces[at].append(tripled(piece, 1))
    smooth = dot(jnp.concatenate(pieces[0] + pieces[1], axis=0), smooth_z)
    deriv = dot(jnp.concatenate(pieces[2], axis=0), deriv_z)
    number = len(some)
    return [
        [smooth[at * count : (at + 1) * count] for at in range(number)],
        [smooth[(number + at) * count : (number + at + 1) * count] for at in range(number)],
        [deriv[at * count : (at + 1) * count] for at in range(number)],
    ]


def join_kernel(first, second, both):
    both[: first.shape[0]] = first[...]
    both[first.shape[0] :] = second[...]


def load_kernel(
    spread_far, tables_far, own_tables_far, back_z_far, forward_far, inverse_far,
    spread, tables, own_tables, back_z, forward, inverse, sems,
):
    gx, gy = 2 * lax.axis_index("pair") + lax.axis_index("core"), lax.axis_index("gy")
    copies = [
        pltpu.make_async_copy(source, target, sems.at[at])
        for at, (source, target) in enumerate((
            (spread_far, spread), (tables_far, tables), (own_tables_far.at[gx], own_tables), (back_z_far, back_z),
            (forward_far, forward), (inverse_far.at[gy], inverse),
        ))
    ]
    for copy in copies:
        copy.start()
    for copy in copies:
        copy.wait()


def inner_kernel(
    own, swapped, crossed, bands, scale_row, momenta_far, partial, smooth_x, deriv_x, momenta, sems, *, group, radius
):
    _, rows, cols, depth = partial.shape
    arriving = [
        pltpu.make_async_copy(momenta_far.at[component], momenta.at[component], sems.at[component])
        for component in range(3)
    ]
    for copy in arriving:
        copy.start()
    places, _ = band_rows(rows, cols, depth, radius)
    along_x, own_y, smooth_z, deriv_z = [band(bands, places, n) for n in ("x", "own", "smooth", "deriv")]
    along_first(
        [lambda col=col: [x[pl.ds(col, rows, stride=cols), :] for x in (own, swapped, crossed)] for col in range(cols)],
        along_x, smooth_x, deriv_x,
    )
    for start in range(0, rows, group):
        short = along_others(
            smooth_x, deriv_x, range(start, start + group), rows, cols, own_y, smooth_z, deriv_z
        )
        for component in range(3):
            for at in range(group):
                partial[component, start + at] = short[component][at]
    scale = scale_row[0:1, :]
    for component in range(3):
        arriving[component].wait()
        for row in range(rows):
            partial[component, row] = momenta[component, row] + scale * partial[component, row]


def cut_kernel(tile, strip):
    radius = strip.shape[1]
    strip[...] = tile[:, pl.ds(side_start(1, radius, tile.shape[1]), radius), :]


def outer_kernel(
    strip_a, strip_b, besides, cross_a, cross_b, bands, scale_row, base, kicked,
    smooth_x, deriv_x, staged, sems, *, group,
):
    _, rows, cols, depth = base.shape
    radius = strip_a.shape[0] // rows
    places, _ = band_rows(rows, cols, depth, radius)
    along_x, along_y, smooth_z, deriv_z = [band(bands, places, n) for n in ("x", "sides", "smooth", "deriv")]
    along_first(
        [
            lambda start=start, col=col, strip=strip, cross=cross: [
                strip[pl.ds(col, rows, stride=radius), :], besides[pl.ds(start + col, rows, stride=radius), :],
                cross[pl.ds(col, rows, stride=radius), :],
            ]
            for start, strip, cross in ((0, strip_a, cross_a), (rows * radius, strip_b, cross_b))
            for col in range(radius)
        ],
        along_x, smooth_x, deriv_x,
    )
    scale = scale_row[0:1, :]
    copies = []
    for start in range(0, rows, group):
        short = along_others(
            smooth_x, deriv_x, range(start, start + group), rows, 2 * radius, along_y, smooth_z, deriv_z
        )
        for component in range(3):
            for at in range(group):
                row = start + at
                staged[component, row, radius : cols - radius] = base[component, row, radius : cols - radius]
                for which in range(2):
                    side = pl.ds(side_start(which, radius, cols), radius)
                    near = short[component][at][which * radius : (which + 1) * radius]
                    staged[component, row, side] = base[component, row, side] + scale * near
        copies.append(pltpu.make_async_copy(
            staged.at[:, pl.ds(start, group)], kicked.at[:, pl.ds(start, group)], sems.at[start // group]
        ))
        copies[-1].start()
    for copy in copies:
        copy.wait()


def call(body, outs, n_in, scratch=(), smem=(), far=(), near=(), kept=False, spaces=None, mib=8, cost=10**6, alias={}):
    made = pl.pallas_call(
        body,
        out_shape=[
            pltpu.VMEM(s, d) if (kept if isinstance(kept, bool) else kept[at]) else jax.ShapeDtypeStruct(s, d)
            for at, (s, d) in enumerate(outs)
        ],
        in_specs=[SMEM if at in smem else HBM if at in far else VMEM for at in range(n_in)],
        out_specs=spaces or [VMEM for _ in outs],
        scratch_shapes=list(scratch),
        input_output_aliases=alias,
        cost_estimate=pl.CostEstimate(flops=cost, bytes_accessed=cost, transcendentals=0),
        compiler_params=pltpu.CompilerParams(vmem_limit_bytes=mib * 1024 * 1024),
    )

    def run(*operands):
        return made(*[
            pltpu.with_memory_space_constraint(o, pltpu.HBM) if at in far
            else pltpu.with_memory_space_constraint(o, pltpu.VMEM) if at in near else o
            for at, o in enumerate(operands)
        ])

    return run


def per_device(density, momenta, smooth_taps, deriv_taps, kick_step):
    rows, cols, depth = density.shape
    radius = (smooth_taps.shape[0] - 1) // 2
    count_gx, count_gy = 2 * lax.axis_size("pair"), lax.axis_size("gy")
    assert count_gy % 2 == 0 and radius % 16 == 0
    assert rows == radius and cols >= 2 * radius and depth == LANES
    groups, lines, deep = rows // FACTOR, cols // FACTOR, depth // FACTOR
    assert groups == FACTOR and groups * deep == LANES
    coarse_x, coarse_y = groups * count_gx, lines * count_gy
    quads = coarse_x // groups
    assert quads % CHUNK == 0
    assert lines % TILE == 0
    f, b = jnp.float32, jnp.bfloat16

    basis_x, waves_x = real_basis(coarse_x)
    basis_y, waves_y = real_basis(coarse_y)
    basis_z, waves_z = real_basis(deep)

    pool = split_table(np.tile(np.repeat(basis_z.T, FACTOR, 0) / FACTOR**3, (1, groups)), 0)
    _, band_height = band_rows(rows, cols, depth, radius)
    own, bands, send_a, send_b, coarse = call(
        prepare_kernel,
        [((rows, cols, depth), f), ((band_height, LANES), b), ((rows, radius, depth), f), ((rows, radius, depth), f),
         ((count_gx // 2 * count_gy * (lines // TILE), TILE, LANES), f)],
        4,
        [pltpu.VMEM((count_gx // 2 * count_gy * (lines // TILE), TILE, LANES), f), pltpu.VMEM(pool.shape, b),
         pltpu.VMEM((groups * cols, depth), f), pltpu.SMEM(smooth_taps.shape, f), pltpu.SMEM(deriv_taps.shape, f),
         DMA((groups + 6,))],
        far=(0, 1, 2, 3), kept=(True, True, False, False, False), spaces=[VMEM, VMEM, HBM, HBM, HBM],
        mib=8 if count_gx <= CHUNK else 24,
    )(density, jnp.asarray(pool), smooth_taps, deriv_taps)

    def shift(values, pairs):
        return lax.ppermute(values, ("pair", "core", "gy"), [
            (a * count_gy + c, d * count_gy + e) for (a, c), (d, e) in pairs
        ])

    every = [(i, j) for i in range(count_gx) for j in range(count_gy)]
    beside = lambda i: i + 1 if i % 2 == 0 else i - 1
    across = lambda i: (i - 1) % count_gx if i % 2 == 0 else (i + 1) % count_gx
    crossed = shift(density, [((i, j), (across(i), j)) for i, j in every])
    swapped = shift(density, [((i, j), (beside(i), j)) for i, j in every])
    pair_a = lambda j: j + 1 if j % 2 == 0 else j - 1
    pair_b = lambda j: (j + 1) % count_gy if j % 2 == 1 else (j - 1) % count_gy
    strip_a = shift(send_a, [((i, j), (i, pair_a(j))) for i, j in every])
    strip_b = shift(send_b, [((i, j), (i, pair_b(j))) for i, j in every])
    cross_a = shift(strip_a, [((i, j), (across(i), j)) for i, j in every])
    (crossed_b,) = call(cut_kernel, [((rows, radius, depth), f)], 1, near=(0,), kept=True)(crossed)
    cross_b = shift(crossed_b, [((i, j), (i, pair_b(j))) for i, j in every])

    blocks = lax.all_to_all(coarse, ("pair", "gy"), split_axis=0, concat_axis=0, tiled=True)
    beside_blocks = shift(blocks, [((i, j), (beside(i), j)) for i, j in every])

    scale = jnp.broadcast_to(kick_step, (8, LANES))
    spread = np.zeros((quads, count_gx, groups, groups, deep))
    for turn in range(groups):
        for j in range(groups):
            for quad in range(quads):
                spread[quad, :, turn, j, :] = basis_x[quad * groups + j].reshape(count_gx, groups)[
                    :, (j + turn) % groups
                ][:, None]
    back_y = np.concatenate([
        np.repeat(t.T.reshape(count_gy, lines, coarse_y), FACTOR, 1) for t in (basis_y, centred(basis_y))
    ], 1)
    back_x = np.stack([basis_x, centred(basis_x)])
    back_x = back_x.reshape(2, quads, groups, count_gx, groups).transpose(3, 1, 0, 4, 2)
    back_x = np.repeat(back_x[..., None], deep, -1).reshape(count_gx, -1, LANES)
    back_z = np.stack([
        np.tile(np.repeat(t, FACTOR, 1), (groups, 1)) * LONG_COUPLING for t in (basis_z, centred(basis_z))
    ])
    other = (eigenvalues(waves_x, coarse_x).reshape(quads, groups, 1) + eigenvalues(waves_z, deep)).reshape(
        quads, LANES
    )
    second = np.repeat(eigenvalues(waves_y, coarse_y)[:, None], LANES, 1)
    far_tables = [
        spread.reshape(-1, LANES).astype(np.float32),
        np.concatenate([second, other]).astype(np.float32), back_x.astype(np.float32),
        split_table(back_z, 1), split_table(basis_y, 1), split_table(back_y, 2),
    ]

    (joined,) = call(join_kernel, [((2 * rows, radius, depth), f)], 2, near=(0, 1), kept=True)(strip_a, strip_b)
    besides = shift(joined, [((i, j), (beside(i), j)) for i, j in every])
    near_tables = [(t.shape[1:] if at in (2, 5) else t.shape, t.dtype) for at, t in enumerate(far_tables)]
    far_tables = [jnp.asarray(t) for t in far_tables]
    small = count_gx <= CHUNK
    near_tables = call(
        load_kernel, near_tables, 6, [DMA((6,))], far=tuple(range(6)), kept=small, mib=8 if small else 52,
    )(*far_tables)
    (partial,) = call(
        functools.partial(inner_kernel, group=GROUP, radius=radius),
        [((3, rows, cols, depth), f)], 6,
        [pltpu.VMEM((rows * cols, depth), f), pltpu.VMEM((rows * cols, depth), f),
         pltpu.VMEM((3, rows, cols, depth), f), DMA((3,))],
        far=(5,), near=(0, 1, 2, 3, 4), kept=True,
    )(*[x.reshape(rows * cols, depth) for x in (own, swapped, crossed)], bands, scale, momenta)
    (base,) = call(
        functools.partial(solve_kernel, lines=lines),
        [((3, rows, cols, depth), f)], 10,
        [pltpu.VMEM((coarse_y, CHUNK * LANES), f), pltpu.VMEM((coarse_x, coarse_y, LANES), f),
         pltpu.VMEM((quads, 2 * cols, LANES), f), pltpu.VMEM((3, groups * cols, LANES), f)],
        near=tuple(range(10)) if small else (), kept=small, mib=8 if small else 52, alias={8: 0},
    )(blocks, beside_blocks, *near_tables, partial, scale)
    strips = [x.reshape(-1, depth) for x in (strip_a, strip_b, besides, cross_a, cross_b)]
    (kicked,) = call(
        functools.partial(outer_kernel, group=SIDE_GROUP), [((3, rows, cols, depth), f)], 8,
        [pltpu.VMEM((2 * rows * radius, depth), f), pltpu.VMEM((2 * rows * radius, depth), f),
         pltpu.VMEM((3, rows, cols, depth), f), DMA((rows // SIDE_GROUP,))],
        near=tuple(range(8)), spaces=[HBM],
    )(*strips, bands, scale, base)
    return kicked


def solution(mesh):
    assert mesh.shape["gx"] % 2 == 0
    count_gx, count_gy = mesh.shape["gx"], mesh.shape["gy"]
    mesh = jax.sharding.Mesh(
        np.asarray(mesh.devices).reshape(count_gx // 2, 2, count_gy), ("pair", "core", "gy")
    )

    gx = ("pair", "core")
    in_specs = (P(gx, "gy", None), P(None, gx, "gy", None), P(), P(), P())
    out_specs = P(None, gx, "gy", None)
    return jax.shard_map(per_device, mesh=mesh, in_specs=in_specs, out_specs=out_specs, check_vma=False)
```
